32 devices in a mesh: dp: 4 (over z), group: 8 (over y, x, core).
Axes of the slice: x: 2, y: 2, z: 4, core: 2. Of those that a mesh axis runs over, the one named last changes fastest.
Arguments:
- qkv: bfloat16 [2048, 1920], P(('dp', 'group')), may hold values from -200 to 200
- embed_grad: bfloat16 [2048, 1280], P(('dp', 'group')), may hold values from -0.59765625 to 0.59765625
- out_weight: bfloat16 [1280, 640], replicated, may hold values from -0.25 to 0.25
- image_len: int32 [4, 8, 8], P('dp'), may hold values from 0 to 8, as said below
- image_order: int32 [4, 8, 8], P('dp', 'group'), may hold values from 0 to 7, each once within a row
- image_cut: int32 [4, 8], P('dp', 'group'), may hold values from 8 to 24
Outputs:
- embeds: bfloat16 [2048, 1280], P(('dp', 'group'))
- qkv_grad: bfloat16 [2048, 1920], P(('dp', 'group'))
- weight_grad: float32 [1280, 640], P('group')
The draws below stay inside these ranges and needn't reach their ends.
Inputs may be any that keep to these rules, and one draw needn't show every extreme that they name: For every replica r and destination d, the sum over sources s of image_len[r, s, d] is exactly 32; 0 means that s sends nothing to d. Each image_order[r, s] names every destination once.
All inputs are finite; a program needn't handle non-finite values.
Results may differ from the reference program's by a relative error of at most 0.017.
Values may be sent and summed in bfloat16 or wider, within the bound.
A program may use at most 64 MiB of HBM per device.

```python
import functools
import math
import jax
import jax.numpy as jnp
from jax import lax

D = 1280
HD = 80
HEADS = 8
SLOT = 8
HF = 640
PACK = 32
SRC_ROWS = 64
ROWS = 2048
N_DP = 4
N_GROUP = 8


def draw_qkv(key, part):
    first = jax.random.fold_in(key, 0)
    base = jnp.clip(jax.random.normal(first, (ROWS, 3 * HF), jnp.float32), -6.0, 6.0)
    return base.astype(jnp.bfloat16)


def draw_image_len(key, part):
    first, second = jax.random.split(key, 2)
    pairs = N_GROUP // 2
    lower = jax.random.randint(first, (N_DP, pairs, 1), 0, SLOT + 1)
    spread = jax.random.randint(second, (N_DP, pairs, N_GROUP), 0, SLOT + 1)
    upper = lower + spread * (SLOT + 1 - lower) // (SLOT + 1)
    pair_index = jnp.arange(pairs, dtype=jnp.int32)[None, :, None]
    dest_index = jnp.arange(N_GROUP, dtype=jnp.int32)[None, None, :]
    upper = jnp.where((pair_index == 0) & (dest_index == 0), SLOT, upper)
    stacked = jnp.stack([upper, SLOT - upper], axis=2)
    return stacked.reshape(N_DP, N_GROUP, N_GROUP).astype(jnp.int32)


def with_ends(array, own_key, smallest, top_value):
    spot = [jax.random.randint(jax.random.fold_in(own_key, axis), (), 0, length) for axis, length in enumerate(array.shape)]
    longest = array.shape.index(max(array.shape))
    neighbour = spot[:longest] + [(spot[longest] + 1) % array.shape[longest]] + spot[longest + 1:]
    return array.at[tuple(spot)].set(smallest).at[tuple(neighbour)].set(top_value)


def raised(drawn, stream_key, source, target, shards_of, factor):
    owner, partner = [(jnp.arange(drawn.shape[dim]) // (drawn.shape[dim] // shards_of)).reshape([-1 if axis == dim else 1 for axis in range(drawn.ndim)]) for dim in (source, target)]
    chosen = jax.random.permutation(stream_key, shards_of)[partner]
    strong = (owner == chosen) | (owner == (partner + shards_of // 2) % shards_of)
    return jnp.where(strong, factor * drawn, drawn)


def steps_of(rng, shape, cuts, smallest, largest):
    loudness, own = 1.0, jax.random.fold_in(rng, 6)
    for dim, blocks in cuts:
        draws = jnp.exp(jax.random.uniform(jax.random.fold_in(own, dim), (blocks,), jnp.float32, smallest / len(cuts), largest / len(cuts)))
        loudness = loudness * jnp.repeat(draws, shape[dim] // blocks).reshape([-1 if axis == dim else 1 for axis in range(len(shape))])
    return loudness


def normal_values(key, extent, deviation, most, pieces=(), kind=jnp.bfloat16):
    values = deviation * jax.random.normal(key, extent, jnp.float32)
    if pieces:
        values = values * steps_of(key, extent, pieces, -0.22, 0.18)
    return jnp.clip(values, -most, most).astype(kind)


def heavy_noise(rng, extent, scale, bound, pieces, heavy, kind=jnp.bfloat16):
    array = scale * jax.random.normal(rng, extent, jnp.float32)
    if pieces:
        array = array * steps_of(rng, extent, pieces, -0.22, 0.18)
    return jnp.clip(raised(array, jax.random.fold_in(rng, 3), *heavy), -bound, bound).astype(kind)


def setup_inputs(seed: int = 0) -> dict:
    seeds = jax.random.split(jax.random.key(seed), 7)
    return {
        "qkv": draw_qkv(jax.random.fold_in(seeds[6], 71), 0),
        "embed_grad": heavy_noise(seeds[1], (ROWS, D), 0.1, 0.59765625, ((0, 32),), (0, 1, 32, 2.75)),
        "out_weight": normal_values(seeds[2], (D, HF), HF ** -0.5, 0.25),
        "image_len": draw_image_len(jax.random.fold_in(seeds[6], 71), 0),
        "image_order": jax.vmap(lambda own: jax.random.permutation(own, N_GROUP))(jax.random.split(seeds[4], N_DP * N_GROUP)).reshape((N_DP, N_GROUP, N_GROUP)).astype(jnp.int32),
        "image_cut": with_ends(jax.random.randint(seeds[5], (N_DP, N_GROUP), N_GROUP * SLOT // 8, 3 * N_GROUP * SLOT // 8 + 1), jax.random.fold_in(seeds[5], 1), N_GROUP * SLOT // 8, (3 * N_GROUP * SLOT // 8 + 1) - 1).astype(jnp.int32),
    }


masked_value = -1e+30

def dest_block(qkv, embed_grad, out_weight, image_len, image_order, image_cut, weight_sum, block):
    replica = (block // N_GROUP).astype(jnp.int32)
    target = (block % N_GROUP).astype(jnp.int32)
    lens = lax.dynamic_index_in_dim(image_len, replica, 0, keepdims=False)
    order = lax.dynamic_index_in_dim(image_order, replica, 0, keepdims=False)
    cut = lax.dynamic_index_in_dim(image_cut.reshape(-1), block, 0, keepdims=False)
    dest_range = jnp.arange(N_GROUP, dtype=jnp.int32)
    onehot = (order[:, :, None] == dest_range[None, None, :]).astype(jnp.int32)
    ordered = lax.optimization_barrier(jnp.sum(onehot * lens[:, None, :], axis=2)).astype(jnp.int32)
    ends = jnp.cumsum(ordered, axis=1).astype(jnp.int32)
    starts = ends - ordered
    dest_start = lax.optimization_barrier(jnp.sum(onehot * starts[:, :, None], axis=1)).astype(jnp.int32)
    column = lax.dynamic_index_in_dim(lens, target, 1, keepdims=False)
    start_col = lax.dynamic_index_in_dim(dest_start, target, 1, keepdims=False)
    col_ends = jnp.cumsum(column).astype(jnp.int32)
    col_starts = col_ends - column
    positions = jnp.arange(PACK, dtype=jnp.int32)
    source_of = lax.optimization_barrier(jnp.sum((col_ends[None, :] <= positions[:, None]).astype(jnp.int32), axis=1)).astype(jnp.int32)
    selector = (source_of[:, None] == dest_range[None, :]).astype(jnp.int32)
    offset = positions - lax.optimization_barrier(jnp.sum(selector * col_starts[None, :], axis=1)).astype(jnp.int32)
    local = lax.optimization_barrier(jnp.sum(selector * start_col[None, :], axis=1)).astype(jnp.int32) + offset
    rows = ((replica * N_GROUP + source_of) * SRC_ROWS + local).astype(jnp.int32)
    qkv_rows = jnp.take(qkv, rows, axis=0)
    cot_rows = jnp.take(embed_grad, rows, axis=0)
    second = positions >= cut
    same = second[:, None] == second[None, :]
    score_scale = 1.0 / math.sqrt(HD)
    query = qkv_rows[:, :HF].astype(jnp.float32).reshape(PACK, HEADS, HD)
    keys = qkv_rows[:, HF:2 * HF].astype(jnp.float32).reshape(PACK, HEADS, HD)
    values = qkv_rows[:, 2 * HF:].astype(jnp.float32).reshape(PACK, HEADS, HD)
    scores = jnp.einsum('qhe,khe->hqk', query, keys) * score_scale
    scores = jnp.where(same[None], scores, masked_value)
    top = lax.optimization_barrier(jnp.max(scores, axis=-1, keepdims=True))
    expo = jnp.exp(scores - top)
    probs = expo / lax.optimization_barrier(jnp.sum(expo, axis=-1, keepdims=True))
    probs_b = probs.astype(jnp.bfloat16)
    attended = jnp.einsum('hqk,khe->qhe', probs_b.astype(jnp.float32), values).astype(jnp.bfloat16)
    attended = attended.reshape(PACK, HF)
    embeds = jnp.dot(attended, out_weight.T, preferred_element_type=jnp.float32).astype(jnp.bfloat16)
    attended_grad = jnp.dot(cot_rows, out_weight, preferred_element_type=jnp.float32).astype(jnp.bfloat16)
    weight_sum = weight_sum + jnp.dot(cot_rows.T, attended, preferred_element_type=jnp.float32)
    grad_heads = attended_grad.astype(jnp.float32).reshape(PACK, HEADS, HD)
    att_heads = attended.astype(jnp.float32).reshape(PACK, HEADS, HD)
    prob_grad = jnp.einsum('qhe,khe->hqk', grad_heads, values)
    delta = jnp.transpose(lax.optimization_barrier(jnp.sum(grad_heads * att_heads, axis=-1)), (1, 0))[:, :, None]
    score_grad = (probs * (prob_grad - delta) * score_scale).astype(jnp.bfloat16).astype(jnp.float32)
    query_grad = jnp.einsum('hqk,khe->qhe', score_grad, keys).astype(jnp.bfloat16)
    keys_grad = jnp.einsum('hqk,qhe->khe', score_grad, query).astype(jnp.bfloat16)
    values_grad = jnp.einsum('hqk,qhe->khe', probs_b.astype(jnp.float32), grad_heads).astype(jnp.bfloat16)
    grads = jnp.concatenate([query_grad.reshape(PACK, HF), keys_grad.reshape(PACK, HF), values_grad.reshape(PACK, HF)], axis=1)
    return (weight_sum, (embeds, grads, rows))

def reference(qkv, embed_grad, out_weight, image_len, image_order, image_cut):
    blocks = jnp.arange(N_DP * N_GROUP, dtype=jnp.int32)
    step_fn = functools.partial(dest_block, qkv, embed_grad, out_weight, image_len, image_order, image_cut)
    weight_sum, outputs = lax.scan(step_fn, jnp.zeros((D, HF), jnp.float32), blocks)
    embeds, grads, rows = outputs
    flat_rows = rows.reshape(-1)
    embeds_all = jnp.zeros((ROWS, D), jnp.bfloat16).at[flat_rows].set(embeds.reshape(-1, D))
    grads_all = jnp.zeros((ROWS, 3 * HF), jnp.bfloat16).at[flat_rows].set(grads.reshape(-1, 3 * HF))
    return (embeds_all, grads_all, weight_sum)
```

```python
import functools
import math

import jax
import jax.numpy as jnp
from jax import lax
from jax.experimental import pallas as pl
from jax.experimental.pallas import tpu as pltpu
from jax.sharding import PartitionSpec as P

HD = 80
HEADS = 8
SLOT = 8
CHUNKS = 5
MASKED = -1e30
F32 = jnp.float32
BF16 = jnp.bfloat16
MESH = pl.DeviceIdType.MESH


def dot(a, b, dims=((1,), (0,))):
    return lax.dot_general(a, b, (dims, ((), ())), preferred_element_type=F32)


TN = ((0,), (0,))
NT = ((1,), (1,))


def iota(shape, dim):
    return lax.broadcasted_iota(jnp.int32, shape, dim)


def flat(x):
    g, s, c = x.shape
    return x.astype(F32).reshape(g * s, c).astype(BF16)


def partner(me, k):
    out, bit = me, 1
    while bit <= k:
        if k & bit:
            has = lax.rem(lax.div(me, bit), 2)
            out = out + bit * (1 - 2 * has)
        bit *= 2
    return out


def kernel(
    groups, reps,
    len_ref, order_ref, cut_ref, qkv_hbm, cot_hbm, w_hbm,
    emb_hbm, grad_hbm, wg_hbm,
    qkv, cot, w, sel, pack_t,
    sendq, recvq, sendg, recvg, cots, cotr, qbig, gbig, attall,
    grads, backs, backr, packed_cot, wgs, own, zsend, zbuf, emb, grad,
    in_sem, out_sem, loc_sem,
    sq, rq, sg, rg, sc, rc, sa, ra, sb, rb, sz, rz,
):
    me = lax.axis_index("group")
    rep = lax.axis_index("dp")
    rows, feats3 = qkv.shape
    hf = feats3 // 3
    width = cot.shape[1]
    slots = groups * SLOT
    pack = slots // 2
    share = width // groups
    tiles = width // 128

    loads = [
        pltpu.make_async_copy(qkv_hbm, qkv, in_sem.at[0]),
        pltpu.make_async_copy(cot_hbm, cot, in_sem.at[1]),
        pltpu.make_async_copy(w_hbm, w, in_sem.at[2]),
    ]
    for load in loads:
        load.start()

    barrier = pltpu.get_barrier_semaphore()
    order_k = list(range(groups - 1, 0, -1))
    for k in order_k:
        pl.semaphore_signal(
            barrier, inc=1, device_id={"group": partner(me, k)}, device_id_type=MESH
        )

    @pl.when(rep > 0)
    def _():
        pl.semaphore_signal(barrier, inc=1, device_id={"dp": rep - 1}, device_id_type=MESH)

    @pl.when(rep < reps - 1)
    def _():
        pl.semaphore_signal(barrier, inc=1, device_id={"dp": rep + 1}, device_id_type=MESH)

    sub = iota((groups, groups), 0)
    lane = iota((groups, groups), 1)
    eye = sub == lane
    lens = len_ref[...].astype(F32)
    lens_row = jnp.sum(jnp.where(sub == me, lens, 0.0), axis=0, keepdims=True)
    order_row = order_ref[...].astype(F32)
    order_col = jnp.sum(
        jnp.where(eye, jnp.broadcast_to(order_row, eye.shape), 0.0), axis=1, keepdims=True
    )
    onehot = jnp.where(order_col == lane.astype(F32), 1.0, 0.0)
    ordered_col = jnp.sum(onehot * lens_row, axis=1, keepdims=True)
    ordered_row = jnp.sum(jnp.where(eye, ordered_col, 0.0), axis=0, keepdims=True)
    starts_col = jnp.sum(
        jnp.where(lane < sub, jnp.broadcast_to(ordered_row, eye.shape), 0.0),
        axis=1, keepdims=True,
    )
    dest_row = jnp.sum(onehot * starts_col, axis=0, keepdims=True)
    block_of = iota((slots, groups), 0) // SLOT == iota((slots, groups), 1)
    within = lax.rem(iota((slots, 1), 0), SLOT).astype(F32)
    send_start = jnp.sum(jnp.where(block_of, dest_row, 0.0), axis=1, keepdims=True)
    send_len = jnp.sum(jnp.where(block_of, lens_row, 0.0), axis=1, keepdims=True)
    send_pos = jnp.where(within < send_len, send_start + within, -1.0)
    sel[...] = jnp.where(send_pos == iota((slots, rows), 1).astype(F32), 1.0, 0.0).astype(BF16)

    before = jnp.where(lane < sub, 1.0, 0.0).astype(BF16)
    lens_b = lens.astype(BF16)
    starts = dot(before, lens_b)
    expand = jnp.where(block_of, 1.0, 0.0).astype(BF16)
    pos_all = dot(expand, starts.astype(BF16)) + within
    pos_all = jnp.where(within < dot(expand, lens_b), pos_all, -1.0)
    lane_sg = iota((slots, groups), 1)
    pos_me = jnp.sum(jnp.where(lane_sg == me, pos_all, 0.0), axis=1, keepdims=True)
    packs = iota((slots, pack), 1).astype(F32)
    pack_t[...] = jnp.where(pos_me == packs, 1.0, 0.0).astype(BF16)

    def remote(src, dst, ssem, rsem, k):
        return pltpu.make_async_remote_copy(
            src_ref=src, dst_ref=dst, send_sem=ssem, recv_sem=rsem,
            device_id={"group": partner(me, k)}, device_id_type=MESH,
        )

    loads[0].wait()
    sendq[...] = dot(sel[...], qkv[...]).reshape(groups, SLOT, feats3).astype(BF16)

    pl.semaphore_wait(
        barrier,
        groups - 1 + (rep > 0).astype(jnp.int32) + (rep < reps - 1).astype(jnp.int32),
    )

    pending = []
    for k in order_k:
        copy = remote(sendq.at[partner(me, k)], recvq.at[me], sq.at[k], rq.at[k], k)
        copy.start()
        pending.append(copy)
    local_q = pltpu.make_async_copy(sendq.at[me], recvq.at[me], loc_sem.at[0])
    local_q.start()

    loads[1].wait()
    loads[2].wait()
    att_grad = dot(cot[...], w[...]).astype(BF16)
    sendg[...] = dot(sel[...], att_grad).reshape(groups, SLOT, hf).astype(BF16)
    pending_g = []
    for k in order_k:
        copy = remote(sendg.at[partner(me, k)], recvg.at[me], sg.at[k], rg.at[k], k)
        copy.start()
        pending_g.append(copy)
    local_g = pltpu.make_async_copy(sendg.at[me], recvg.at[me], loc_sem.at[1])
    local_g.start()

    cots[...] = dot(sel[...], cot[...]).reshape(groups, SLOT, width).astype(BF16)

    def window(owner):
        first = jnp.minimum(lax.div(owner * share, 128), tiles - 2)
        return first * 128

    pending_c = []
    for k in order_k:
        begin = pl.multiple_of(window(partner(me, k)), 128)
        copy = remote(cots.at[:, :, pl.ds(begin, 256)], cotr.at[me], sc.at[k], rc.at[k], k)
        copy.start()
        pending_c.append(copy)
    mine = pl.multiple_of(window(me), 128)
    local_c = pltpu.make_async_copy(
        cots.at[:, :, pl.ds(mine, 256)], cotr.at[me], loc_sem.at[2]
    )
    local_c.start()

    local_q.wait()
    for copy in pending:
        copy.wait_recv()
    xq = dot(pack_t[...], flat(recvq[...]), TN).astype(BF16)
    query, keys, values = xq[:, :hf], xq[:, hf : 2 * hf], xq[:, 2 * hf :]
    feature = iota((1, hf), 1)
    heads = [
        (feature >= h * HD) & (feature < (h + 1) * HD) for h in range(HEADS)
    ]
    marks = [jnp.where(m, 1.0, 0.0).astype(BF16) for m in heads]
    for h in range(HEADS):
        qbig[h * pack : (h + 1) * pack, :] = query * marks[h]
    scale = 1.0 / math.sqrt(HD)
    cut = cut_ref[0, 0]
    wide = HEADS * pack
    row_second = iota((pack, wide), 0) >= cut
    col_second = lax.rem(iota((pack, wide), 1), pack) >= cut
    same = row_second == col_second
    scores = dot(keys, qbig[...], NT) * scale
    scores = jnp.where(same, scores, MASKED)
    top = jnp.max(scores, axis=0, keepdims=True)
    expo = jnp.exp(scores - top)
    probs = expo / jnp.sum(expo, axis=0, keepdims=True)
    probs_b = probs.astype(BF16)

    def per_head(big):
        out = jnp.where(heads[0], big[:pack], 0.0)
        for h in range(1, HEADS):
            out = jnp.where(heads[h], big[h * pack : (h + 1) * pack], out)
        return out.astype(BF16)

    att = per_head(dot(probs_b, values, TN))
    attall[pl.ds(me, 1)] = att.reshape(1, pack, hf)
    pending_a = []
    for k in order_k:
        copy = remote(attall.at[me], attall.at[me], sa.at[k], ra.at[k], k)
        copy.start()
        pending_a.append(copy)
    grads[:, :hf] = att

    local_g.wait()
    for copy in pending_g:
        copy.wait_recv()
    xg = dot(pack_t[...], flat(recvg[...]), TN).astype(BF16)
    for h in range(HEADS):
        gbig[h * pack : (h + 1) * pack, :] = xg * marks[h]
    prob_grad = dot(values, gbig[...], NT)
    delta = jnp.sum(probs * prob_grad, axis=0, keepdims=True)
    score_grad = (probs * (prob_grad - delta) * scale).astype(BF16)
    grads[:, hf : 2 * hf] = per_head(dot(score_grad, keys, TN))
    grads[:, 2 * hf : 3 * hf] = dot(score_grad, qbig[...]).astype(BF16)
    grads[:, 3 * hf :] = dot(probs_b, gbig[...]).astype(BF16)

    backs[...] = dot(pack_t[...], grads[...]).reshape(groups, SLOT, 4 * hf).astype(BF16)
    pending_b = []
    for k in order_k:
        copy = remote(backs.at[partner(me, k)], backr.at[me], sb.at[k], rb.at[k], k)
        copy.start()
        pending_b.append(copy)
    local_b = pltpu.make_async_copy(backs.at[me], backr.at[me], loc_sem.at[3])
    local_b.start()

    local_c.wait()
    for copy in pending_c:
        copy.wait_recv()
    for d in range(groups):
        place = jnp.where(pos_all[:, d : d + 1] == packs, 1.0, 0.0).astype(BF16)
        packed_cot[d * pack : (d + 1) * pack, :] = dot(
            place, flat(cotr[:, d]), TN
        ).astype(BF16)
    for copy in pending_a:
        copy.wait_recv()
    wgs[...] = dot(packed_cot[...], attall[...].reshape(groups * pack, hf), TN)
    offset = pl.multiple_of(me * share - window(me), 8)
    own[...] = wgs[pl.ds(offset, share), :].reshape(own.shape)

    @pl.when(rep == 0)
    def _():
        zbuf[0] = jnp.zeros(zbuf.shape[1:], BF16)

    @pl.when(rep == reps - 1)
    def _():
        zbuf[1] = jnp.zeros(zbuf.shape[1:], BF16)

    def hop(way, c):
        return pltpu.make_async_remote_copy(
            src_ref=zsend.at[way, c], dst_ref=zbuf.at[way, c],
            send_sem=sz.at[way, c], recv_sem=rz.at[way, c],
            device_id={"dp": rep + 1 - 2 * way}, device_id_type=MESH,
        )

    def step(way, c):
        spot = rep + way * (reps - 1 - 2 * rep)

        @pl.when(spot > 0)
        def _():
            hop(way, c).wait_recv()

        @pl.when(spot < reps - 1)
        def _():
            zsend[way, c] = (own[c] + zbuf[way, c].astype(F32)).astype(BF16)
            hop(way, c).start()

    near = (rep >= reps // 2).astype(jnp.int32)
    lag = 2
    for t in range(CHUNKS + lag):
        if t < CHUNKS:
            step(near, t)
        if t >= lag:
            step(1 - near, t - lag)

    local_b.wait()
    for copy in pending_b:
        copy.wait_recv()
    back = dot(sel[...], flat(backr[...]), TN).astype(BF16)
    grad[...] = back[:, hf:]
    store_g = pltpu.make_async_copy(grad, grad_hbm, out_sem.at[1])
    store_g.start()
    emb[...] = dot(back[:, :hf], w[...], NT).astype(BF16)
    store_e = pltpu.make_async_copy(emb, emb_hbm, out_sem.at[0])
    store_e.start()

    own[...] = own[...] + zbuf[0].astype(F32) + zbuf[1].astype(F32)
    store_w = pltpu.make_async_copy(own, wg_hbm, out_sem.at[2])
    store_w.start()

    for copies in (pending, pending_g, pending_c, pending_a, pending_b):
        for copy in copies:
            copy.wait_send()
    for way in range(2):
        spot = rep + way * (reps - 1 - 2 * rep)

        @pl.when(spot < reps - 1)
        def _():
            for c in range(CHUNKS):
                hop(way, c).wait_send()

    store_g.wait()
    store_e.wait()
    store_w.wait()


def local(groups, reps, qkv, embed_grad, out_weight, image_len, image_order, image_cut):
    rows, feats3 = qkv.shape
    width, hf = out_weight.shape
    slots = groups * SLOT
    pack = slots // 2
    share = width // groups
    part = share // CHUNKS
    any_space = pl.BlockSpec(memory_space=pl.ANY)
    vmem = pl.BlockSpec(memory_space=pltpu.VMEM)
    smem = pl.BlockSpec(memory_space=pltpu.SMEM)
    dma = pltpu.SemaphoreType.DMA
    emb, grad, wg = pl.pallas_call(
        functools.partial(kernel, groups, reps),
        out_shape=(
            jax.ShapeDtypeStruct((rows, width), BF16),
            jax.ShapeDtypeStruct((rows, feats3), BF16),
            jax.ShapeDtypeStruct((CHUNKS, part, hf), F32),
        ),
        in_specs=[vmem, vmem, smem, any_space, any_space, any_space],
        out_specs=(any_space, any_space, any_space),
        scratch_shapes=[
            pltpu.VMEM((rows, feats3), BF16),
            pltpu.VMEM((rows, width), BF16),
            pltpu.VMEM((width, hf), BF16),
            pltpu.VMEM((slots, rows), BF16),
            pltpu.VMEM((slots, pack), BF16),
            pltpu.VMEM((groups, SLOT, feats3), BF16),
            pltpu.VMEM((groups, SLOT, feats3), BF16),
            pltpu.VMEM((groups, SLOT, hf), BF16),
            pltpu.VMEM((groups, SLOT, hf), BF16),
            pltpu.VMEM((groups, SLOT, width), BF16),
            pltpu.VMEM((groups, groups, SLOT, 256), BF16),
            pltpu.VMEM((HEADS * pack, hf), BF16),
            pltpu.VMEM((HEADS * pack, hf), BF16),
            pltpu.VMEM((groups, pack, hf), BF16),
            pltpu.VMEM((pack, 4 * hf), BF16),
            pltpu.VMEM((groups, SLOT, 4 * hf), BF16),
            pltpu.VMEM((groups, SLOT, 4 * hf), BF16),
            pltpu.VMEM((groups * pack, 256), BF16),
            pltpu.VMEM((256, hf), F32),
            pltpu.VMEM((CHUNKS, part, hf), F32),
            pltpu.VMEM((2, CHUNKS, part, hf), BF16),
            pltpu.VMEM((2, CHUNKS, part, hf), BF16),
            pltpu.VMEM((rows, width), BF16),
            pltpu.VMEM((rows, feats3), BF16),
            dma((3,)), dma((3,)), dma((4,)),
        ]
        + [dma((groups,)) for _ in range(10)]
        + [dma((2, CHUNKS)), dma((2, CHUNKS))],
        compiler_params=pltpu.CompilerParams(
            collective_id=0, has_side_effects=True, vmem_limit_bytes=60 * 1024 * 1024
        ),
    )(
        image_len.reshape(groups, groups), image_order.reshape(1, groups), image_cut,
        qkv, embed_grad, out_weight,
    )
    return emb, grad, wg.reshape(share, hf)


def solution(mesh):
    return jax.shard_map(
        functools.partial(local, mesh.shape["group"], mesh.shape["dp"]),
        mesh=mesh,
        in_specs=(
            P(("dp", "group"), None),
            P(("dp", "group"), None),
            P(),
            P("dp", None, None),
            P("dp", "group", None),
            P("dp", "group"),
        ),
        out_specs=(P(("dp", "group"), None), P(("dp", "group"), None), P("group", None)),
        check_vma=False,
    )
```

```python
import functools
import math

import jax
import jax.numpy as jnp
from jax import lax
from jax.experimental import pallas as pl
from jax.experimental.pallas import tpu as pltpu
from jax.sharding import PartitionSpec as P

HD = 80
HEADS = 8
SLOT = 8
CHUNKS = 5
MASKED = -1e30
F32 = jnp.float32
BF16 = jnp.bfloat16
MESH = pl.DeviceIdType.MESH


TRACE = False
open_scope = []


def mark(name):
    if TRACE:
        if open_scope:
            open_scope.pop().__exit__(None, None, None)
        if name:
            scope = jax.named_scope(name)
            scope.__enter__()
            open_scope.append(scope)


def dot(a, b, dims=((1,), (0,))):
    return lax.dot_general(a, b, (dims, ((), ())), preferred_element_type=F32)


TN = ((0,), (0,))
NT = ((1,), (1,))


def iota(shape, dim):
    return lax.broadcasted_iota(jnp.int32, shape, dim)


def flat(x):
    g, s, c = x.shape
    return x.astype(F32).reshape(g * s, c).astype(BF16)


def partner(me, k):
    out, bit = me, 1
    while bit <= k:
        if k & bit:
            has = lax.rem(lax.div(me, bit), 2)
            out = out + bit * (1 - 2 * has)
        bit *= 2
    return out


def kernel(
    groups, reps,
    len_ref, order_ref, cut_ref, qkv_hbm, cot_hbm, w_hbm,
    emb, grad, own,
    qkv, cot, w, sel, pack_t,
    sendq, recvq, sendg, recvg, cots, cotr, qbig, gbig, attall,
    grads, backs, backr, packed_cot, wgs, zsend, zbuf,
    in_sem, loc_sem,
    sq, rq, sg, rg, sc, rc, sa, ra, sb, rb, sz, rz,
):
    me = lax.axis_index("group")
    rep = lax.axis_index("dp")
    rows, feats3 = qkv.shape
    hf = feats3 // 3
    width = cot.shape[1]
    slots = groups * SLOT
    pack = slots // 2
    share = width // groups
    tiles = width // 128

    mark("m00_start")
    loads = [
        pltpu.make_async_copy(qkv_hbm, qkv, in_sem.at[0]),
        pltpu.make_async_copy(cot_hbm, cot, in_sem.at[1]),
        pltpu.make_async_copy(w_hbm, w, in_sem.at[2]),
    ]
    for load in loads:
        load.start()

    barrier = pltpu.get_barrier_semaphore()
    order_k = list(range(groups - 1, 0, -1))
    for k in order_k:
        pl.semaphore_signal(
            barrier, inc=1, device_id={"group": partner(me, k)}, device_id_type=MESH
        )

    @pl.when(rep > 0)
    def _():
        pl.semaphore_signal(barrier, inc=1, device_id={"dp": rep - 1}, device_id_type=MESH)

    @pl.when(rep < reps - 1)
    def _():
        pl.semaphore_signal(barrier, inc=1, device_id={"dp": rep + 1}, device_id_type=MESH)

    mark("m01_book")
    sub = iota((groups, groups), 0)
    lane = iota((groups, groups), 1)
    eye = sub == lane
    lens = len_ref[...].astype(F32)
    lens_row = jnp.sum(jnp.where(sub == me, lens, 0.0), axis=0, keepdims=True)
    order_row = order_ref[...].astype(F32)
    order_col = jnp.sum(
        jnp.where(eye, jnp.broadcast_to(order_row, eye.shape), 0.0), axis=1, keepdims=True
    )
    onehot = jnp.where(order_col == lane.astype(F32), 1.0, 0.0)
    ordered_col = jnp.sum(onehot * lens_row, axis=1, keepdims=True)
    ordered_row = jnp.sum(jnp.where(eye, ordered_col, 0.0), axis=0, keepdims=True)
    starts_col = jnp.sum(
        jnp.where(lane < sub, jnp.broadcast_to(ordered_row, eye.shape), 0.0),
        axis=1, keepdims=True,
    )
    dest_row = jnp.sum(onehot * starts_col, axis=0, keepdims=True)
    block_of = iota((slots, groups), 0) // SLOT == iota((slots, groups), 1)
    within = lax.rem(iota((slots, 1), 0), SLOT).astype(F32)
    send_start = jnp.sum(jnp.where(block_of, dest_row, 0.0), axis=1, keepdims=True)
    send_len = jnp.sum(jnp.where(block_of, lens_row, 0.0), axis=1, keepdims=True)
    send_pos = jnp.where(within < send_len, send_start + within, -1.0)
    sel[...] = jnp.where(send_pos == iota((slots, rows), 1).astype(F32), 1.0, 0.0).astype(BF16)

    before = jnp.where(lane < sub, 1.0, 0.0).astype(BF16)
    lens_b = lens.astype(BF16)
    starts = dot(before, lens_b)
    expand = jnp.where(block_of, 1.0, 0.0).astype(BF16)
    pos_all = dot(expand, starts.astype(BF16)) + within
    pos_all = jnp.where(within < dot(expand, lens_b), pos_all, -1.0)
    lane_sg = iota((slots, groups), 1)
    pos_me = jnp.sum(jnp.where(lane_sg == me, pos_all, 0.0), axis=1, keepdims=True)
    packs = iota((slots, pack), 1).astype(F32)
    pack_t[...] = jnp.where(pos_me == packs, 1.0, 0.0).astype(BF16)

    def remote(src, dst, ssem, rsem, k):
        return pltpu.make_async_remote_copy(
            src_ref=src, dst_ref=dst, send_sem=ssem, recv_sem=rsem,
            device_id={"group": partner(me, k)}, device_id_type=MESH,
        )

    mark("m02_selq")
    loads[0].wait()
    sendq[...] = dot(sel[...], qkv[...]).reshape(groups, SLOT, feats3).astype(BF16)

    mark("m03_barrier")
    pl.semaphore_wait(
        barrier,
        groups - 1 + (rep > 0).astype(jnp.int32) + (rep < reps - 1).astype(jnp.int32),
    )

    mark("m04_sendq")
    pending = []
    for k in order_k:
        copy = remote(sendq.at[partner(me, k)], recvq.at[me], sq.at[k], rq.at[k], k)
        copy.start()
        pending.append(copy)
    local_q = pltpu.make_async_copy(sendq.at[me], recvq.at[me], loc_sem.at[0])
    local_q.start()

    mark("m05_attgrad")
    loads[1].wait()
    loads[2].wait()
    att_grad = dot(cot[...], w[...]).astype(BF16)
    sendg[...] = dot(sel[...], att_grad).reshape(groups, SLOT, hf).astype(BF16)
    pending_g = []
    for k in order_k:
        copy = remote(sendg.at[partner(me, k)], recvg.at[me], sg.at[k], rg.at[k], k)
        copy.start()
        pending_g.append(copy)
    local_g = pltpu.make_async_copy(sendg.at[me], recvg.at[me], loc_sem.at[1])
    local_g.start()

    mark("m06_cot")
    cots[...] = dot(sel[...], cot[...]).reshape(groups, SLOT, width).astype(BF16)

    def window(owner):
        first = jnp.minimum(lax.div(owner * share, 128), tiles - 2)
        return first * 128

    pending_c = []
    for k in order_k:
        begin = pl.multiple_of(window(partner(me, k)), 128)
        copy = remote(cots.at[:, :, pl.ds(begin, 256)], cotr.at[me], sc.at[k], rc.at[k], k)
        copy.start()
        pending_c.append(copy)
    mine = pl.multiple_of(window(me), 128)
    local_c = pltpu.make_async_copy(
        cots.at[:, :, pl.ds(mine, 256)], cotr.at[me], loc_sem.at[2]
    )
    local_c.start()

    mark("m07_waitq")
    local_q.wait()
    for copy in pending:
        copy.wait_recv()
    mark("m08_att")
    xq = dot(pack_t[...], flat(recvq[...]), TN).astype(BF16)
    query, keys, values = xq[:, :hf], xq[:, hf : 2 * hf], xq[:, 2 * hf :]
    feature = iota((1, hf), 1)
    heads = [
        (feature >= h * HD) & (feature < (h + 1) * HD) for h in range(HEADS)
    ]
    marks = [jnp.where(m, 1.0, 0.0).astype(BF16) for m in heads]
    for h in range(HEADS):
        qbig[h * pack : (h + 1) * pack, :] = query * marks[h]
    scale = 1.0 / math.sqrt(HD)
    cut = cut_ref[0, 0]
    wide = HEADS * pack
    row_second = iota((pack, wide), 0) >= cut
    col_second = lax.rem(iota((pack, wide), 1), pack) >= cut
    same = row_second == col_second
    scores = dot(keys, qbig[...], NT) * scale
    scores = jnp.where(same, scores, MASKED)
    top = jnp.max(scores, axis=0, keepdims=True)
    expo = jnp.exp(scores - top)
    probs = expo / jnp.sum(expo, axis=0, keepdims=True)
    probs_b = probs.astype(BF16)

    def per_head(big):
        out = jnp.where(heads[0], big[:pack], 0.0)
        for h in range(1, HEADS):
            out = jnp.where(heads[h], big[h * pack : (h + 1) * pack], out)
        return out.astype(BF16)

    att = per_head(dot(probs_b, values, TN))
    attall[pl.ds(me, 1)] = att.reshape(1, pack, hf)
    pending_a = []
    for k in order_k:
        copy = remote(attall.at[me], attall.at[me], sa.at[k], ra.at[k], k)
        copy.start()
        pending_a.append(copy)
    grads[:, :hf] = att

    mark("m09_waitg")
    local_g.wait()
    for copy in pending_g:
        copy.wait_recv()
    mark("m10_bwd")
    xg = dot(pack_t[...], flat(recvg[...]), TN).astype(BF16)
    for h in range(HEADS):
        gbig[h * pack : (h + 1) * pack, :] = xg * marks[h]
    prob_grad = dot(values, gbig[...], NT)
    delta = jnp.sum(probs * prob_grad, axis=0, keepdims=True)
    score_grad = (probs * (prob_grad - delta) * scale).astype(BF16)
    grads[:, hf : 2 * hf] = per_head(dot(score_grad, keys, TN))
    grads[:, 2 * hf : 3 * hf] = dot(score_grad, qbig[...]).astype(BF16)
    grads[:, 3 * hf :] = dot(probs_b, gbig[...]).astype(BF16)

    backs[...] = dot(pack_t[...], grads[...]).reshape(groups, SLOT, 4 * hf).astype(BF16)
    pending_b = []
    for k in order_k:
        copy = remote(backs.at[partner(me, k)], backr.at[me], sb.at[k], rb.at[k], k)
        copy.start()
        pending_b.append(copy)
    local_b = pltpu.make_async_copy(backs.at[me], backr.at[me], loc_sem.at[3])
    local_b.start()

    mark("m11_waitc")
    local_c.wait()
    for copy in pending_c:
        copy.wait_recv()
    mark("m12_pack")
    for d in range(groups):
        place = jnp.where(pos_all[:, d : d + 1] == packs, 1.0, 0.0).astype(BF16)
        packed_cot[d * pack : (d + 1) * pack, :] = dot(
            place, flat(cotr[:, d]), TN
        ).astype(BF16)
    mark("m13_waita")
    for copy in pending_a:
        copy.wait_recv()
    mark("m14_wg")
    wgs[...] = dot(packed_cot[...], attall[...].reshape(groups * pack, hf), TN)
    offset = pl.multiple_of(me * share - window(me), 8)
    own[...] = wgs[pl.ds(offset, share), :].reshape(own.shape)

    mark("m15_zchain")
    @pl.when(rep == 0)
    def _():
        zbuf[0] = jnp.zeros(zbuf.shape[1:], BF16)

    @pl.when(rep == reps - 1)
    def _():
        zbuf[1] = jnp.zeros(zbuf.shape[1:], BF16)

    def hop(way, c):
        return pltpu.make_async_remote_copy(
            src_ref=zsend.at[way, c], dst_ref=zbuf.at[way, c],
            send_sem=sz.at[way, c], recv_sem=rz.at[way, c],
            device_id={"dp": rep + 1 - 2 * way}, device_id_type=MESH,
        )

    def step(way, c):
        spot = rep + way * (reps - 1 - 2 * rep)

        @pl.when(spot > 0)
        def _():
            hop(way, c).wait_recv()

        @pl.when(spot < reps - 1)
        def _():
            zsend[way, c] = (own[c] + zbuf[way, c].astype(F32)).astype(BF16)
            hop(way, c).start()

    def source_rows():
        mark("m16_waitb")
        local_b.wait()
        for copy in pending_b:
            copy.wait_recv()
        mark("m17_back")
        back = dot(sel[...], flat(backr[...]), TN).astype(BF16)
        grad[...] = back[:, hf:]
        emb[...] = dot(back[:, :hf], w[...], NT).astype(BF16)
        mark("m175")

    near = (rep >= (reps + 1) // 2).astype(jnp.int32)
    edge = (rep == 0) | (rep == reps - 1)

    @pl.when(edge)
    def _():
        for c in range(CHUNKS):
            step(near, c)
        source_rows()
        for c in range(CHUNKS):
            step(1 - near, c)

    @pl.when(jnp.logical_not(edge))
    def _():
        lag = 2
        for t in range(CHUNKS + lag):
            if t < CHUNKS:
                step(near, t)
            if t >= lag:
                step(1 - near, t - lag)
        source_rows()

    mark("m18_final")
    own[...] = own[...] + zbuf[0].astype(F32) + zbuf[1].astype(F32)

    mark("m19_drain")
    for copies in (pending, pending_g, pending_c, pending_a, pending_b):
        for copy in copies:
            copy.wait_send()
    for way in range(2):
        spot = rep + way * (reps - 1 - 2 * rep)

        @pl.when(spot < reps - 1)
        def _():
            for c in range(CHUNKS):
                hop(way, c).wait_send()

    mark(None)


def write_out(emb, grad, own, emb_hbm, grad_hbm, wg_hbm, sems):
    pairs = ((emb, emb_hbm), (grad, grad_hbm), (own, wg_hbm))
    copies = [
        pltpu.make_async_copy(src, dst, sems.at[i]) for i, (src, dst) in enumerate(pairs)
    ]
    for copy in copies:
        copy.start()
    for copy in copies:
        copy.wait()


def local(groups, reps, qkv, embed_grad, out_weight, image_len, image_order, image_cut):
    rows, feats3 = qkv.shape
    width, hf = out_weight.shape
    slots = groups * SLOT
    pack = slots // 2
    share = width // groups
    part = share // CHUNKS
    any_space = pl.BlockSpec(memory_space=pl.ANY)
    vmem = pl.BlockSpec(memory_space=pltpu.VMEM)
    smem = pl.BlockSpec(memory_space=pltpu.SMEM)
    dma = pltpu.SemaphoreType.DMA
    emb, grad, wg = pl.pallas_call(
        functools.partial(kernel, groups, reps),
        out_shape=(
            pltpu.VMEM((rows, width), BF16),
            pltpu.VMEM((rows, feats3), BF16),
            pltpu.VMEM((CHUNKS, part, hf), F32),
        ),
        in_specs=[vmem, vmem, smem, any_space, any_space, any_space],
        out_specs=(vmem, vmem, vmem),
        scratch_shapes=[
            pltpu.VMEM((rows, feats3), BF16),
            pltpu.VMEM((rows, width), BF16),
            pltpu.VMEM((width, hf), BF16),
            pltpu.VMEM((slots, rows), BF16),
            pltpu.VMEM((slots, pack), BF16),
            pltpu.VMEM((groups, SLOT, feats3), BF16),
            pltpu.VMEM((groups, SLOT, feats3), BF16),
            pltpu.VMEM((groups, SLOT, hf), BF16),
            pltpu.VMEM((groups, SLOT, hf), BF16),
            pltpu.VMEM((groups, SLOT, width), BF16),
            pltpu.VMEM((groups, groups, SLOT, 256), BF16),
            pltpu.VMEM((HEADS * pack, hf), BF16),
            pltpu.VMEM((HEADS * pack, hf), BF16),
            pltpu.VMEM((groups, pack, hf), BF16),
            pltpu.VMEM((pack, 4 * hf), BF16),
            pltpu.VMEM((groups, SLOT, 4 * hf), BF16),
            pltpu.VMEM((groups, SLOT, 4 * hf), BF16),
            pltpu.VMEM((groups * pack, 256), BF16),
            pltpu.VMEM((256, hf), F32),
            pltpu.VMEM((2, CHUNKS, part, hf), BF16),
            pltpu.VMEM((2, CHUNKS, part, hf), BF16),
            dma((3,)), dma((4,)),
        ]
        + [dma((groups,)) for _ in range(10)]
        + [dma((2, CHUNKS)), dma((2, CHUNKS))],
        compiler_params=pltpu.CompilerParams(
            collective_id=0, has_side_effects=True, vmem_limit_bytes=60 * 1024 * 1024
        ),
    )(
        image_len.reshape(groups, groups), image_order.reshape(1, groups), image_cut,
        qkv, embed_grad, out_weight,
    )
    emb, grad, wg = pl.pallas_call(
        write_out,
        out_shape=(
            jax.ShapeDtypeStruct((rows, width), BF16),
            jax.ShapeDtypeStruct((rows, feats3), BF16),
            jax.ShapeDtypeStruct((CHUNKS, part, hf), F32),
        ),
        in_specs=[vmem, vmem, vmem],
        out_specs=(any_space, any_space, any_space),
        scratch_shapes=[dma((3,))],
    )(*(pltpu.with_memory_space_constraint(x, pltpu.VMEM) for x in (emb, grad, wg)))
    return emb, grad, wg.reshape(share, hf)


def solution(mesh):
    return jax.shard_map(
        functools.partial(local, mesh.shape["group"], mesh.shape["dp"]),
        mesh=mesh,
        in_specs=(
            P(("dp", "group"), None),
            P(("dp", "group"), None),
            P(),
            P("dp", None, None),
            P("dp", "group", None),
            P("dp", "group"),
        ),
        out_specs=(P(("dp", "group"), None), P(("dp", "group"), None), P("group", None)),
        check_vma=False,
    )
```

```python
import functools
import math

import jax
import jax.numpy as jnp
from jax import lax
from jax.experimental import pallas as pl
from jax.experimental.pallas import tpu as pltpu
from jax.sharding import PartitionSpec as P

HD = 80
HEADS = 8
SLOT = 8
MASKED = -1e30
F32 = jnp.float32
BF16 = jnp.bfloat16
MESH = pl.DeviceIdType.MESH


TRACE = False
open_scope = []


def mark(name):
    if TRACE:
        if open_scope:
            open_scope.pop().__exit__(None, None, None)
        if name:
            scope = jax.named_scope(name)
            scope.__enter__()
            open_scope.append(scope)


def dot(a, b, dims=((1,), (0,))):
    return lax.dot_general(a, b, (dims, ((), ())), preferred_element_type=F32)


TN = ((0,), (0,))
NT = ((1,), (1,))


def iota(shape, dim):
    return lax.broadcasted_iota(jnp.int32, shape, dim)


def flat(x):
    g, s, c = x.shape
    return x.astype(F32).reshape(g * s, c).astype(BF16)


def partner(me, k):
    out, bit = me, 1
    while bit <= k:
        if k & bit:
            has = lax.rem(lax.div(me, bit), 2)
            out = out + bit * (1 - 2 * has)
        bit *= 2
    return out


def kernel(
    groups, reps,
    len_hbm, order_hbm, cut_hbm, qkv_hbm, cot_hbm, w_hbm,
    emb, grad, own,
    len_ref, order_ref, cut_ref, qkv, cot, w, sel, pack_t,
    sendq, recvq, sendg, recvg, cots, cotr, qbig, gbig, attall,
    grads, backs, backr, packed_cot, wgs, zsend, zbuf,
    in_sem, loc_sem,
    sq, rq, sg, rg, sc, rc, sa, ra, sb, rb, sz, rz,
):
    me = lax.axis_index("group")
    rep = lax.axis_index("dp")
    rows, feats3 = qkv.shape
    hf = feats3 // 3
    width = cot.shape[1]
    slots = groups * SLOT
    pack = slots // 2
    share = width // groups
    tiles = width // 128
    chunks = zbuf.shape[1]

    mark("m00_start")
    barrier = pltpu.get_barrier_semaphore()
    order_k = list(range(groups - 1, 0, -1))
    for k in order_k:
        pl.semaphore_signal(
            barrier, inc=1, device_id={"group": partner(me, k)}, device_id_type=MESH
        )

    @pl.when(rep > 0)
    def _():
        pl.semaphore_signal(barrier, inc=1, device_id={"dp": rep - 1}, device_id_type=MESH)

    @pl.when(rep < reps - 1)
    def _():
        pl.semaphore_signal(barrier, inc=1, device_id={"dp": rep + 1}, device_id_type=MESH)

    loads = [
        pltpu.make_async_copy(src, dst, in_sem.at[i])
        for i, (src, dst) in enumerate(
            (
                (qkv_hbm, qkv), (cot_hbm, cot), (w_hbm, w),
                (len_hbm, len_ref), (order_hbm, order_ref), (cut_hbm, cut_ref),
            )
        )
    ]
    for i in (3, 4, 5, 0, 1, 2):
        loads[i].start()

    mark("m01_book")
    for i in (3, 4, 5):
        loads[i].wait()
    sub = iota((groups, groups), 0)
    lane = iota((groups, groups), 1)
    eye = sub == lane
    lens = len_ref[...].astype(F32)
    lens_row = jnp.sum(jnp.where(sub == me, lens, 0.0), axis=0, keepdims=True)
    order_row = order_ref[...].astype(F32)
    order_col = jnp.sum(
        jnp.where(eye, jnp.broadcast_to(order_row, eye.shape), 0.0), axis=1, keepdims=True
    )
    onehot = jnp.where(order_col == lane.astype(F32), 1.0, 0.0)
    ordered_col = jnp.sum(onehot * lens_row, axis=1, keepdims=True)
    ordered_row = jnp.sum(jnp.where(eye, ordered_col, 0.0), axis=0, keepdims=True)
    starts_col = jnp.sum(
        jnp.where(lane < sub, jnp.broadcast_to(ordered_row, eye.shape), 0.0),
        axis=1, keepdims=True,
    )
    dest_row = jnp.sum(onehot * starts_col, axis=0, keepdims=True)
    block_of = iota((slots, groups), 0) // SLOT == iota((slots, groups), 1)
    within = lax.rem(iota((slots, 1), 0), SLOT).astype(F32)
    send_start = jnp.sum(jnp.where(block_of, dest_row, 0.0), axis=1, keepdims=True)
    send_len = jnp.sum(jnp.where(block_of, lens_row, 0.0), axis=1, keepdims=True)
    send_pos = jnp.where(within < send_len, send_start + within, -1.0)
    sel[...] = jnp.where(send_pos == iota((slots, rows), 1).astype(F32), 1.0, 0.0).astype(BF16)

    before = jnp.where(lane < sub, 1.0, 0.0).astype(BF16)
    lens_b = lens.astype(BF16)
    starts = dot(before, lens_b)
    expand = jnp.where(block_of, 1.0, 0.0).astype(BF16)
    pos_all = dot(expand, starts.astype(BF16)) + within
    pos_all = jnp.where(within < dot(expand, lens_b), pos_all, -1.0)
    lane_sg = iota((slots, groups), 1)
    pos_me = jnp.sum(jnp.where(lane_sg == me, pos_all, 0.0), axis=1, keepdims=True)
    packs = iota((slots, pack), 1).astype(F32)
    pack_t[...] = jnp.where(pos_me == packs, 1.0, 0.0).astype(BF16)

    def remote(src, dst, ssem, rsem, k):
        return pltpu.make_async_remote_copy(
            src_ref=src, dst_ref=dst, send_sem=ssem, recv_sem=rsem,
            device_id={"group": partner(me, k)}, device_id_type=MESH,
        )

    mark("m02_selq")
    loads[0].wait()
    sendq[...] = dot(sel[...], qkv[...]).reshape(groups, SLOT, feats3).astype(BF16)

    mark("m03_barrier")
    pl.semaphore_wait(
        barrier,
        groups - 1 + (rep > 0).astype(jnp.int32) + (rep < reps - 1).astype(jnp.int32),
    )

    mark("m04_sendq")
    pending = []
    for k in order_k:
        copy = remote(sendq.at[partner(me, k)], recvq.at[me], sq.at[k], rq.at[k], k)
        copy.start()
        pending.append(copy)
    local_q = pltpu.make_async_copy(sendq.at[me], recvq.at[me], loc_sem.at[0])
    local_q.start()

    mark("m05_attgrad")
    loads[1].wait()
    loads[2].wait()
    att_grad = dot(cot[...], w[...]).astype(BF16)
    sendg[...] = dot(sel[...], att_grad).reshape(groups, SLOT, hf).astype(BF16)
    pending_g = []
    for k in order_k:
        copy = remote(sendg.at[partner(me, k)], recvg.at[me], sg.at[k], rg.at[k], k)
        copy.start()
        pending_g.append(copy)
    local_g = pltpu.make_async_copy(sendg.at[me], recvg.at[me], loc_sem.at[1])
    local_g.start()

    mark("m06_cot")
    cots[...] = dot(sel[...], cot[...]).reshape(groups, SLOT, width).astype(BF16)

    def window(owner):
        first = jnp.minimum(lax.div(owner * share, 128), tiles - 2)
        return first * 128

    pending_c = []
    for k in order_k:
        begin = pl.multiple_of(window(partner(me, k)), 128)
        copy = remote(cots.at[:, :, pl.ds(begin, 256)], cotr.at[me], sc.at[k], rc.at[k], k)
        copy.start()
        pending_c.append(copy)
    mine = pl.multiple_of(window(me), 128)
    local_c = pltpu.make_async_copy(
        cots.at[:, :, pl.ds(mine, 256)], cotr.at[me], loc_sem.at[2]
    )
    local_c.start()

    mark("m07_waitq")
    local_q.wait()
    for copy in pending:
        copy.wait_recv()
    mark("m08_att")
    xq = dot(pack_t[...], flat(recvq[...]), TN).astype(BF16)
    query, keys, values = xq[:, :hf], xq[:, hf : 2 * hf], xq[:, 2 * hf :]
    feature = iota((1, hf), 1)
    heads = [
        (feature >= h * HD) & (feature < (h + 1) * HD) for h in range(HEADS)
    ]
    marks = [jnp.where(m, 1.0, 0.0).astype(BF16) for m in heads]
    for h in range(HEADS):
        qbig[h * pack : (h + 1) * pack, :] = query * marks[h]
    scale = 1.0 / math.sqrt(HD)
    cut = cut_ref[...]
    wide = HEADS * pack
    row_second = iota((pack, wide), 0) >= cut
    col_second = lax.rem(iota((pack, wide), 1), pack) >= cut
    same = row_second == col_second
    scores = dot(keys, qbig[...], NT) * scale
    scores = jnp.where(same, scores, MASKED)
    top = jnp.max(scores, axis=0, keepdims=True)
    expo = jnp.exp(scores - top)
    probs = expo / jnp.sum(expo, axis=0, keepdims=True)
    probs_b = probs.astype(BF16)

    def per_head(big):
        out = jnp.where(heads[0], big[:pack], 0.0)
        for h in range(1, HEADS):
            out = jnp.where(heads[h], big[h * pack : (h + 1) * pack], out)
        return out.astype(BF16)

    att = per_head(dot(probs_b, values, TN))
    attall[pl.ds(me, 1)] = att.reshape(1, pack, hf)
    pending_a = []
    for k in list(range(groups - 2, 0, -2)) + [1]:
        copy = remote(attall.at[me], attall.at[me], sa.at[k], ra.at[k], k)
        copy.start()
        pending_a.append(copy)
    grads[:, :hf] = att

    mark("m09_waitg")
    local_g.wait()
    for copy in pending_g:
        copy.wait_recv()
    mark("m10_bwd")
    xg = dot(pack_t[...], flat(recvg[...]), TN).astype(BF16)
    for h in range(HEADS):
        gbig[h * pack : (h + 1) * pack, :] = xg * marks[h]
    prob_grad = dot(values, gbig[...], NT)
    delta = jnp.sum(probs * prob_grad, axis=0, keepdims=True)
    score_grad = (probs * (prob_grad - delta) * scale).astype(BF16)
    grads[:, hf : 2 * hf] = per_head(dot(score_grad, keys, TN))
    grads[:, 2 * hf : 3 * hf] = dot(score_grad, qbig[...]).astype(BF16)
    grads[:, 3 * hf :] = dot(probs_b, gbig[...]).astype(BF16)

    backs[...] = dot(pack_t[...], grads[...]).reshape(groups, SLOT, 4 * hf).astype(BF16)
    pending_b = []
    for k in order_k:
        copy = remote(backs.at[partner(me, k)], backr.at[me], sb.at[k], rb.at[k], k)
        copy.start()
        pending_b.append(copy)
    local_b = pltpu.make_async_copy(backs.at[me], backr.at[me], loc_sem.at[3])
    local_b.start()

    mark("m11_waitc")
    local_c.wait()
    for copy in pending_c:
        copy.wait_recv()
    mark("m12_pack")
    for d in range(groups):
        place = jnp.where(pos_all[:, d : d + 1] == packs, 1.0, 0.0).astype(BF16)
        packed_cot[d * pack : (d + 1) * pack, :] = dot(
            place, flat(cotr[:, d]), TN
        ).astype(BF16)
    mark("m13_waita")
    relayed = []
    for k in range(2, groups, 2):
        remote(attall.at[me], attall.at[me], sa.at[k], ra.at[k], k).wait_recv()
        piece = attall.at[partner(me, k)]
        copy = remote(piece, piece, sa.at[k + 1], ra.at[k + 1], 1)
        copy.start()
        relayed.append(copy)
    remote(attall.at[me], attall.at[me], sa.at[1], ra.at[1], 1).wait_recv()
    for copy in relayed:
        copy.wait_recv()
    mark("m14_wg")
    wgs[...] = dot(packed_cot[...], attall[...].reshape(groups * pack, hf), TN)
    offset = pl.multiple_of(me * share - window(me), 8)
    own[...] = wgs[pl.ds(offset, share), :].reshape(own.shape)

    mark("m15_zchain")
    @pl.when(rep == 0)
    def _():
        zbuf[0] = jnp.zeros(zbuf.shape[1:], BF16)

    @pl.when(rep == reps - 1)
    def _():
        zbuf[1] = jnp.zeros(zbuf.shape[1:], BF16)

    def hop(way, c):
        return pltpu.make_async_remote_copy(
            src_ref=zsend.at[way, c], dst_ref=zbuf.at[way, c],
            send_sem=sz.at[way, c], recv_sem=rz.at[way, c],
            device_id={"dp": rep + 1 - 2 * way}, device_id_type=MESH,
        )

    def step(way, c):
        spot = rep + way * (reps - 1 - 2 * rep)

        @pl.when(spot > 0)
        def _():
            hop(way, c).wait_recv()

        @pl.when(spot < reps - 1)
        def _():
            zsend[way, c] = (own[c] + zbuf[way, c].astype(F32)).astype(BF16)
            hop(way, c).start()

    def source_rows():
        mark("m16_waitb")
        local_b.wait()
        for copy in pending_b:
            copy.wait_recv()
        mark("m17_back")
        back = dot(sel[...], flat(backr[...]), TN).astype(BF16)
        grad[...] = back[:, hf:]
        emb[...] = dot(back[:, :hf], w[...], NT).astype(BF16)
        mark("m175")

    near = (rep >= (reps + 1) // 2).astype(jnp.int32)
    edge = (rep == 0) | (rep == reps - 1)

    @pl.when(edge)
    def _():
        for c in range(chunks):
            step(near, c)
        source_rows()
        for c in range(chunks):
            step(1 - near, c)

    @pl.when(jnp.logical_not(edge))
    def _():
        lag = chunks // 2
        for t in range(chunks + lag):
            if t < chunks:
                step(near, t)
            if t >= lag:
                step(1 - near, t - lag)
        source_rows()

    mark("m18_final")
    own[...] = own[...] + zbuf[0].astype(F32) + zbuf[1].astype(F32)

    mark("m19_drain")
    for copies in (pending, pending_g, pending_c, pending_a, relayed, pending_b):
        for copy in copies:
            copy.wait_send()
    for way in range(2):
        spot = rep + way * (reps - 1 - 2 * rep)

        @pl.when(spot < reps - 1)
        def _():
            for c in range(chunks):
                hop(way, c).wait_send()

    mark(None)


def write_out(emb, grad, own, emb_hbm, grad_hbm, wg_hbm, sems):
    pairs = ((emb, emb_hbm), (grad, grad_hbm), (own, wg_hbm))
    copies = [
        pltpu.make_async_copy(src, dst, sems.at[i]) for i, (src, dst) in enumerate(pairs)
    ]
    for copy in copies:
        copy.start()
    for copy in copies:
        copy.wait()


def local(groups, reps, qkv, embed_grad, out_weight, image_len, image_order, image_cut):
    rows, feats3 = qkv.shape
    width, hf = out_weight.shape
    slots = groups * SLOT
    pack = slots // 2
    share = width // groups
    part = 16 if share % 16 == 0 else 8
    chunks = share // part
    any_space = pl.BlockSpec(memory_space=pl.ANY)
    vmem = pl.BlockSpec(memory_space=pltpu.VMEM)
    dma = pltpu.SemaphoreType.DMA
    emb, grad, wg = pl.pallas_call(
        functools.partial(kernel, groups, reps),
        out_shape=(
            pltpu.VMEM((rows, width), BF16),
            pltpu.VMEM((rows, feats3), BF16),
            pltpu.VMEM((chunks, part, hf), F32),
        ),
        in_specs=[any_space] * 6,
        out_specs=(vmem, vmem, vmem),
        scratch_shapes=[
            pltpu.VMEM((groups, groups), jnp.int32),
            pltpu.VMEM((1, groups), jnp.int32),
            pltpu.VMEM((1, 1), jnp.int32),
            pltpu.VMEM((rows, feats3), BF16),
            pltpu.VMEM((rows, width), BF16),
            pltpu.VMEM((width, hf), BF16),
            pltpu.VMEM((slots, rows), BF16),
            pltpu.VMEM((slots, pack), BF16),
            pltpu.VMEM((groups, SLOT, feats3), BF16),
            pltpu.VMEM((groups, SLOT, feats3), BF16),
            pltpu.VMEM((groups, SLOT, hf), BF16),
            pltpu.VMEM((groups, SLOT, hf), BF16),
            pltpu.VMEM((groups, SLOT, width), BF16),
            pltpu.VMEM((groups, groups, SLOT, 256), BF16),
            pltpu.VMEM((HEADS * pack, hf), BF16),
            pltpu.VMEM((HEADS * pack, hf), BF16),
            pltpu.VMEM((groups, pack, hf), BF16),
            pltpu.VMEM((pack, 4 * hf), BF16),
            pltpu.VMEM((groups, SLOT, 4 * hf), BF16),
            pltpu.VMEM((groups, SLOT, 4 * hf), BF16),
            pltpu.VMEM((groups * pack, 256), BF16),
            pltpu.VMEM((256, hf), F32),
            pltpu.VMEM((2, chunks, part, hf), BF16),
            pltpu.VMEM((2, chunks, part, hf), BF16),
            dma((6,)), dma((4,)),
        ]
        + [dma((groups,)) for _ in range(10)]
        + [dma((2, chunks)), dma((2, chunks))],
        compiler_params=pltpu.CompilerParams(
            collective_id=0, has_side_effects=True, vmem_limit_bytes=60 * 1024 * 1024
        ),
    )(
        image_len.reshape(groups, groups), image_order.reshape(1, groups), image_cut,
        qkv, embed_grad, out_weight,
    )
    emb, grad, wg = pl.pallas_call(
        write_out,
        out_shape=(
            jax.ShapeDtypeStruct((rows, width), BF16),
            jax.ShapeDtypeStruct((rows, feats3), BF16),
            jax.ShapeDtypeStruct((chunks, part, hf), F32),
        ),
        in_specs=[vmem, vmem, vmem],
        out_specs=(any_space, any_space, any_space),
        scratch_shapes=[dma((3,))],
    )(*(pltpu.with_memory_space_constraint(x, pltpu.VMEM) for x in (emb, grad, wg)))
    return emb, grad, wg.reshape(share, hf)


def solution(mesh):
    return jax.shard_map(
        functools.partial(local, mesh.shape["group"], mesh.shape["dp"]),
        mesh=mesh,
        in_specs=(
            P(("dp", "group"), None),
            P(("dp", "group"), None),
            P(),
            P("dp", None, None),
            P("dp", "group", None),
            P("dp", "group"),
        ),
        out_specs=(P(("dp", "group"), None), P(("dp", "group"), None), P("group", None)),
        check_vma=False,
    )
```

```python
import functools
import math

import jax
import jax.numpy as jnp
from jax import lax
from jax.experimental import pallas as pl
from jax.experimental.pallas import tpu as pltpu
from jax.sharding import PartitionSpec as P

HD = 80
HEADS = 8
SLOT = 8
MASKED = -1e30
F32 = jnp.float32
BF16 = jnp.bfloat16
MESH = pl.DeviceIdType.MESH


TRACE = False
open_scope = []


def mark(name):
    if TRACE:
        if open_scope:
            open_scope.pop().__exit__(None, None, None)
        if name:
            scope = jax.named_scope(name)
            scope.__enter__()
            open_scope.append(scope)


def dot(a, b, dims=((1,), (0,))):
    return lax.dot_general(a, b, (dims, ((), ())), preferred_element_type=F32)


TN = ((0,), (0,))
NT = ((1,), (1,))


def iota(shape, dim):
    return lax.broadcasted_iota(jnp.int32, shape, dim)


def flat(x):
    g, s, c = x.shape
    return x.astype(F32).reshape(g * s, c).astype(BF16)


def partner(me, k):
    out, bit = me, 1
    while bit <= k:
        if k & bit:
            has = lax.rem(lax.div(me, bit), 2)
            out = out + bit * (1 - 2 * has)
        bit *= 2
    return out


def kernel(
    groups, reps,
    len_hbm, order_hbm, cut_hbm, qkv_hbm, cot_hbm, w_hbm,
    emb, grad, own,
    len_ref, order_ref, cut_ref, qkv, cot, w, sel, pack_t,
    sendq, recvq, sendg, recvg, cots, cotr, qbig, gbig, attall,
    grads, backs, backr, packed_cot, wgs, zsend, zbuf,
    in_sem, loc_sem,
    sq, rq, sg, rg, sc, rc, sa, ra, sb, rb, sz, rz,
):
    me = lax.axis_index("group")
    rep = lax.axis_index("dp")
    rows, feats3 = qkv.shape
    hf = feats3 // 3
    width = cot.shape[1]
    slots = groups * SLOT
    pack = slots // 2
    share = width // groups
    tiles = width // 128
    chunks = zbuf.shape[1]

    mark("m00_start")
    barrier = pltpu.get_barrier_semaphore()
    order_k = list(range(groups - 1, 0, -1))
    for k in order_k:
        pl.semaphore_signal(
            barrier, inc=1, device_id={"group": partner(me, k)}, device_id_type=MESH
        )

    @pl.when(rep > 0)
    def _():
        pl.semaphore_signal(barrier, inc=1, device_id={"dp": rep - 1}, device_id_type=MESH)

    @pl.when(rep < reps - 1)
    def _():
        pl.semaphore_signal(barrier, inc=1, device_id={"dp": rep + 1}, device_id_type=MESH)

    loads = [
        pltpu.make_async_copy(src, dst, in_sem.at[i])
        for i, (src, dst) in enumerate(
            (
                (qkv_hbm, qkv), (cot_hbm, cot), (w_hbm, w),
                (len_hbm, len_ref), (order_hbm, order_ref), (cut_hbm, cut_ref),
            )
        )
    ]
    for i in (3, 4, 5, 0, 1, 2):
        loads[i].start()

    mark("m01_book")
    for i in (3, 4, 5):
        loads[i].wait()
    sub = iota((groups, groups), 0)
    lane = iota((groups, groups), 1)
    eye = sub == lane
    lens = len_ref[...].astype(F32)
    lens_row = jnp.sum(jnp.where(sub == me, lens, 0.0), axis=0, keepdims=True)
    order_row = order_ref[...].astype(F32)
    order_col = jnp.sum(
        jnp.where(eye, jnp.broadcast_to(order_row, eye.shape), 0.0), axis=1, keepdims=True
    )
    onehot = jnp.where(order_col == lane.astype(F32), 1.0, 0.0)
    ordered_col = jnp.sum(onehot * lens_row, axis=1, keepdims=True)
    ordered_row = jnp.sum(jnp.where(eye, ordered_col, 0.0), axis=0, keepdims=True)
    starts_col = jnp.sum(
        jnp.where(lane < sub, jnp.broadcast_to(ordered_row, eye.shape), 0.0),
        axis=1, keepdims=True,
    )
    dest_row = jnp.sum(onehot * starts_col, axis=0, keepdims=True)
    block_of = iota((slots, groups), 0) // SLOT == iota((slots, groups), 1)
    within = lax.rem(iota((slots, 1), 0), SLOT).astype(F32)
    send_start = jnp.sum(jnp.where(block_of, dest_row, 0.0), axis=1, keepdims=True)
    send_len = jnp.sum(jnp.where(block_of, lens_row, 0.0), axis=1, keepdims=True)
    send_pos = jnp.where(within < send_len, send_start + within, -1.0)
    sel[...] = jnp.where(send_pos == iota((slots, rows), 1).astype(F32), 1.0, 0.0).astype(BF16)

    before = jnp.where(lane < sub, 1.0, 0.0).astype(BF16)
    lens_b = lens.astype(BF16)
    starts = dot(before, lens_b)
    expand = jnp.where(block_of, 1.0, 0.0).astype(BF16)
    pos_all = dot(expand, starts.astype(BF16)) + within
    pos_all = jnp.where(within < dot(expand, lens_b), pos_all, -1.0)
    lane_sg = iota((slots, groups), 1)
    pos_me = jnp.sum(jnp.where(lane_sg == me, pos_all, 0.0), axis=1, keepdims=True)
    packs = iota((slots, pack), 1).astype(F32)
    pack_t[...] = jnp.where(pos_me == packs, 1.0, 0.0).astype(BF16)

    def remote(src, dst, ssem, rsem, k):
        return pltpu.make_async_remote_copy(
            src_ref=src, dst_ref=dst, send_sem=ssem, recv_sem=rsem,
            device_id={"group": partner(me, k)}, device_id_type=MESH,
        )

    mark("m02_selq")
    loads[0].wait()
    sendq[...] = dot(sel[...], qkv[...]).reshape(groups, SLOT, feats3).astype(BF16)

    mark("m03_barrier")
    pl.semaphore_wait(
        barrier,
        groups - 1 + (rep > 0).astype(jnp.int32) + (rep < reps - 1).astype(jnp.int32),
    )

    mark("m04_sendq")
    pending = []
    for k in order_k:
        copy = remote(sendq.at[partner(me, k)], recvq.at[me], sq.at[k], rq.at[k], k)
        copy.start()
        pending.append(copy)
    local_q = pltpu.make_async_copy(sendq.at[me], recvq.at[me], loc_sem.at[0])
    local_q.start()

    mark("m05_attgrad")
    loads[1].wait()
    loads[2].wait()
    att_grad = dot(cot[...], w[...]).astype(BF16)
    sendg[...] = dot(sel[...], att_grad).reshape(groups, SLOT, hf).astype(BF16)
    mark("m06_cot")
    cots[...] = dot(sel[...], cot[...]).reshape(groups, SLOT, width).astype(BF16)

    def window(owner):
        first = jnp.minimum(lax.div(owner * share, 128), tiles - 2)
        return first * 128

    pending_c = []
    for k in order_k:
        begin = pl.multiple_of(window(partner(me, k)), 128)
        copy = remote(cots.at[:, :, pl.ds(begin, 256)], cotr.at[me], sc.at[k], rc.at[k], k)
        copy.start()
        pending_c.append(copy)
    mine = pl.multiple_of(window(me), 128)
    local_c = pltpu.make_async_copy(
        cots.at[:, :, pl.ds(mine, 256)], cotr.at[me], loc_sem.at[2]
    )
    local_c.start()

    mark("m07_waitq")
    local_q.wait()
    for copy in pending:
        copy.wait_recv()
    mark("m08_att")
    xq = dot(pack_t[...], flat(recvq[...]), TN).astype(BF16)
    query, keys, values = xq[:, :hf], xq[:, hf : 2 * hf], xq[:, 2 * hf :]
    feature = iota((1, hf), 1)
    heads = [
        (feature >= h * HD) & (feature < (h + 1) * HD) for h in range(HEADS)
    ]
    marks = [jnp.where(m, 1.0, 0.0).astype(BF16) for m in heads]
    for h in range(HEADS):
        qbig[h * pack : (h + 1) * pack, :] = query * marks[h]
    scale = 1.0 / math.sqrt(HD)
    cut = cut_ref[...]
    wide = HEADS * pack
    row_second = iota((pack, wide), 0) >= cut
    col_second = lax.rem(iota((pack, wide), 1), pack) >= cut
    same = row_second == col_second
    scores = dot(keys, qbig[...], NT) * scale
    scores = jnp.where(same, scores, MASKED)
    top = jnp.max(scores, axis=0, keepdims=True)
    expo = jnp.exp(scores - top)
    probs = expo / jnp.sum(expo, axis=0, keepdims=True)
    probs_b = probs.astype(BF16)

    def per_head(big):
        out = jnp.where(heads[0], big[:pack], 0.0)
        for h in range(1, HEADS):
            out = jnp.where(heads[h], big[h * pack : (h + 1) * pack], out)
        return out.astype(BF16)

    att = per_head(dot(probs_b, values, TN))
    attall[pl.ds(me, 1)] = att.reshape(1, pack, hf)
    pending_a = []
    for k in list(range(groups - 2, 0, -2)) + [1]:
        copy = remote(attall.at[me], attall.at[me], sa.at[k], ra.at[k], k)
        copy.start()
        pending_a.append(copy)
    pending_g = []
    for k in order_k:
        copy = remote(sendg.at[partner(me, k)], recvg.at[me], sg.at[k], rg.at[k], k)
        copy.start()
        pending_g.append(copy)
    local_g = pltpu.make_async_copy(sendg.at[me], recvg.at[me], loc_sem.at[1])
    local_g.start()

    grads[:, :hf] = att

    mark("m11_waitc")
    local_c.wait()
    for copy in pending_c:
        copy.wait_recv()
    mark("m12_pack")
    for d in range(groups):
        place = jnp.where(pos_all[:, d : d + 1] == packs, 1.0, 0.0).astype(BF16)
        packed_cot[d * pack : (d + 1) * pack, :] = dot(
            place, flat(cotr[:, d]), TN
        ).astype(BF16)
    mark("m13_waita")
    relayed = []
    for k in range(2, groups, 2):
        remote(attall.at[me], attall.at[me], sa.at[k], ra.at[k], k).wait_recv()
        piece = attall.at[partner(me, k)]
        copy = remote(piece, piece, sa.at[k + 1], ra.at[k + 1], 1)
        copy.start()
        relayed.append(copy)
    remote(attall.at[me], attall.at[me], sa.at[1], ra.at[1], 1).wait_recv()
    for copy in relayed:
        copy.wait_recv()
    mark("m14_wg")
    wgs[...] = dot(packed_cot[...], attall[...].reshape(groups * pack, hf), TN)
    offset = pl.multiple_of(me * share - window(me), 8)
    own[...] = wgs[pl.ds(offset, share), :].reshape(own.shape)

    mark("m15_zchain")
    @pl.when(rep == 0)
    def _():
        zbuf[0] = jnp.zeros(zbuf.shape[1:], BF16)

    @pl.when(rep == reps - 1)
    def _():
        zbuf[1] = jnp.zeros(zbuf.shape[1:], BF16)

    def hop(way, c):
        return pltpu.make_async_remote_copy(
            src_ref=zsend.at[way, c], dst_ref=zbuf.at[way, c],
            send_sem=sz.at[way, c], recv_sem=rz.at[way, c],
            device_id={"dp": rep + 1 - 2 * way}, device_id_type=MESH,
        )

    def step(way, c):
        spot = rep + way * (reps - 1 - 2 * rep)

        @pl.when(spot > 0)
        def _():
            hop(way, c).wait_recv()

        @pl.when(spot < reps - 1)
        def _():
            zsend[way, c] = (own[c] + zbuf[way, c].astype(F32)).astype(BF16)
            hop(way, c).start()

    near = (rep >= (reps + 1) // 2).astype(jnp.int32)
    edge = (rep == 0) | (rep == reps - 1)

    @pl.when(edge)
    def _():
        for c in range(chunks):
            step(near, c)

    mark("m09_waitg")
    local_g.wait()
    for copy in pending_g:
        copy.wait_recv()
    mark("m10_bwd")
    xg = dot(pack_t[...], flat(recvg[...]), TN).astype(BF16)
    for h in range(HEADS):
        gbig[h * pack : (h + 1) * pack, :] = xg * marks[h]
    prob_grad = dot(values, gbig[...], NT)
    delta = jnp.sum(probs * prob_grad, axis=0, keepdims=True)
    score_grad = (probs * (prob_grad - delta) * scale).astype(BF16)
    grads[:, hf : 2 * hf] = per_head(dot(score_grad, keys, TN))
    grads[:, 2 * hf : 3 * hf] = dot(score_grad, qbig[...]).astype(BF16)
    grads[:, 3 * hf :] = dot(probs_b, gbig[...]).astype(BF16)

    backs[...] = dot(pack_t[...], grads[...]).reshape(groups, SLOT, 4 * hf).astype(BF16)
    pending_b = []
    for k in order_k:
        copy = remote(backs.at[partner(me, k)], backr.at[me], sb.at[k], rb.at[k], k)
        copy.start()
        pending_b.append(copy)
    local_b = pltpu.make_async_copy(backs.at[me], backr.at[me], loc_sem.at[3])
    local_b.start()

    def source_rows():
        mark("m16_waitb")
        local_b.wait()
        for copy in pending_b:
            copy.wait_recv()
        mark("m17_back")
        back = dot(sel[...], flat(backr[...]), TN).astype(BF16)
        grad[...] = back[:, hf:]
        emb[...] = dot(back[:, :hf], w[...], NT).astype(BF16)
        mark("m175")

    @pl.when(edge)
    def _():
        source_rows()
        for c in range(chunks):
            step(1 - near, c)

    @pl.when(jnp.logical_not(edge))
    def _():
        lag = chunks // 2
        for t in range(chunks + lag):
            if t < chunks:
                step(near, t)
            if t >= lag:
                step(1 - near, t - lag)
        source_rows()

    mark("m18_final")
    own[...] = own[...] + zbuf[0].astype(F32) + zbuf[1].astype(F32)

    mark("m19_drain")
    for copies in (pending, pending_g, pending_c, pending_a, relayed, pending_b):
        for copy in copies:
            copy.wait_send()
    for way in range(2):
        spot = rep + way * (reps - 1 - 2 * rep)

        @pl.when(spot < reps - 1)
        def _():
            for c in range(chunks):
                hop(way, c).wait_send()

    mark(None)


def write_out(emb, grad, own, emb_hbm, grad_hbm, wg_hbm, sems):
    pairs = ((emb, emb_hbm), (grad, grad_hbm), (own, wg_hbm))
    copies = [
        pltpu.make_async_copy(src, dst, sems.at[i]) for i, (src, dst) in enumerate(pairs)
    ]
    for copy in copies:
        copy.start()
    for copy in copies:
        copy.wait()


def local(groups, reps, qkv, embed_grad, out_weight, image_len, image_order, image_cut):
    rows, feats3 = qkv.shape
    width, hf = out_weight.shape
    slots = groups * SLOT
    pack = slots // 2
    share = width // groups
    part = 16 if share % 16 == 0 else 8
    chunks = share // part
    any_space = pl.BlockSpec(memory_space=pl.ANY)
    vmem = pl.BlockSpec(memory_space=pltpu.VMEM)
    dma = pltpu.SemaphoreType.DMA
    emb, grad, wg = pl.pallas_call(
        functools.partial(kernel, groups, reps),
        out_shape=(
            pltpu.VMEM((rows, width), BF16),
            pltpu.VMEM((rows, feats3), BF16),
            pltpu.VMEM((chunks, part, hf), F32),
        ),
        in_specs=[any_space] * 6,
        out_specs=(vmem, vmem, vmem),
        scratch_shapes=[
            pltpu.VMEM((groups, groups), jnp.int32),
            pltpu.VMEM((1, groups), jnp.int32),
            pltpu.VMEM((1, 1), jnp.int32),
            pltpu.VMEM((rows, feats3), BF16),
            pltpu.VMEM((rows, width), BF16),
            pltpu.VMEM((width, hf), BF16),
            pltpu.VMEM((slots, rows), BF16),
            pltpu.VMEM((slots, pack), BF16),
            pltpu.VMEM((groups, SLOT, feats3), BF16),
            pltpu.VMEM((groups, SLOT, feats3), BF16),
            pltpu.VMEM((groups, SLOT, hf), BF16),
            pltpu.VMEM((groups, SLOT, hf), BF16),
            pltpu.VMEM((groups, SLOT, width), BF16),
            pltpu.VMEM((groups, groups, SLOT, 256), BF16),
            pltpu.VMEM((HEADS * pack, hf), BF16),
            pltpu.VMEM((HEADS * pack, hf), BF16),
            pltpu.VMEM((groups, pack, hf), BF16),
            pltpu.VMEM((pack, 4 * hf), BF16),
            pltpu.VMEM((groups, SLOT, 4 * hf), BF16),
            pltpu.VMEM((groups, SLOT, 4 * hf), BF16),
            pltpu.VMEM((groups * pack, 256), BF16),
            pltpu.VMEM((256, hf), F32),
            pltpu.VMEM((2, chunks, part, hf), BF16),
            pltpu.VMEM((2, chunks, part, hf), BF16),
            dma((6,)), dma((4,)),
        ]
        + [dma((groups,)) for _ in range(10)]
        + [dma((2, chunks)), dma((2, chunks))],
        compiler_params=pltpu.CompilerParams(
            collective_id=0, has_side_effects=True, vmem_limit_bytes=60 * 1024 * 1024
        ),
    )(
        image_len.reshape(groups, groups), image_order.reshape(1, groups), image_cut,
        qkv, embed_grad, out_weight,
    )
    emb, grad, wg = pl.pallas_call(
        write_out,
        out_shape=(
            jax.ShapeDtypeStruct((rows, width), BF16),
            jax.ShapeDtypeStruct((rows, feats3), BF16),
            jax.ShapeDtypeStruct((chunks, part, hf), F32),
        ),
        in_specs=[vmem, vmem, vmem],
        out_specs=(any_space, any_space, any_space),
        scratch_shapes=[dma((3,))],
    )(*(pltpu.with_memory_space_constraint(x, pltpu.VMEM) for x in (emb, grad, wg)))
    return emb, grad, wg.reshape(share, hf)


def solution(mesh):
    return jax.shard_map(
        functools.partial(local, mesh.shape["group"], mesh.shape["dp"]),
        mesh=mesh,
        in_specs=(
            P(("dp", "group"), None),
            P(("dp", "group"), None),
            P(),
            P("dp", None, None),
            P("dp", "group", None),
            P("dp", "group"),
        ),
        out_specs=(P(("dp", "group"), None), P(("dp", "group"), None), P("group", None)),
        check_vma=False,
    )
```
